256 devices in a mesh: mem: 16 (over y_lo, z), lat: 4 (over x), lon: 4 (over y_hi, core).
Axes of the slice: x: 4, y: 4 (y_hi: 2, y_lo: 2; y = y_hi * 2 + y_lo), z: 8, core: 2. Of those that a mesh axis runs over, the one named last changes fastest.
Arguments:
- ensemble: bfloat16 [256, 73, 32, 512], P('mem', None, 'lat', 'lon'), may hold values from -6 to 6
- ancestry: int32 [256], replicated, may hold values from 0 to 255, as said below
- obs_weights: float32 [256], P('mem'), may hold values from 0.1 to 10
- kernel_index: int32 [32], P('lat'), may hold values from 0 to 7
- kernel_table: float32 [8, 9, 73], replicated, may hold values from -3 to 3
- feature_scaling_factor: float32 [73], replicated, may hold values from 0.1 to 1.9
- entry_projection_matrix: bfloat16 [1536, 73], replicated, may hold values from -0.75 to 0.75
- exit_projection_matrix: bfloat16 [73, 1536], replicated, may hold values from -0.15625 to 0.15625
Outputs:
- predicted_particles: bfloat16 [256, 73, 32, 512], P('mem', None, 'lat', 'lon')
- importance_average_state: float32 [73, 32, 512], P(None, 'lat', 'lon')
The draws below stay inside these ranges and needn't reach their ends.
Inputs may be any that keep to these rules, and one draw needn't show every extreme that they name: `ancestry`: each slot's ancestor member. The slots held by one index of mem take at most 1 distinct ancestors from the members held by any one index of mem.
All inputs are finite; a program needn't handle non-finite values.
Results may differ from the reference program's by a relative error of at most 0.0042.
Values may be sent and summed in bfloat16 or wider, within the bound.
No kernel may reach another device: no remote copies, remote signals or barrier semaphores. Data moves between devices by JAX's collectives and lax.ppermute only.
A program may use at most 128 MiB of HBM per device.

```python
import math
import jax
import jax.numpy as jnp
from jax import lax

C = 73
HID = 1536
KERN = 8
MEM_DEV = 16
CAP = 1
MEM = 256
NLAT = 32
NLON = 512


def draw_ancestry(key, part):
    blocks = MEM // MEM_DEV
    key_one, key_two, key_three, key_four = jax.random.split(key, 4)
    first_pick = jax.random.randint(key_one, (MEM,), 0, blocks)
    second_pick = jax.random.randint(key_two, (MEM,), 0, blocks)
    source_block = jnp.minimum(first_pick, second_pick)
    within_pick = jax.random.randint(key_three, (MEM,), 0, CAP)
    offsets = jax.random.randint(key_four, (blocks, blocks), 0, MEM_DEV)
    slot_ids = jnp.arange(MEM, dtype=jnp.int32)
    dest_block = slot_ids // MEM_DEV
    slot_within = slot_ids % MEM_DEV
    forced = (dest_block == 0) & (slot_within < CAP)
    source_block = jnp.where(forced, 0, source_block)
    within_pick = jnp.where(forced, slot_within, within_pick)
    member_ids = source_block * MEM_DEV + (offsets[dest_block, source_block] + within_pick) % MEM_DEV
    return member_ids.astype(jnp.int32)


def with_ends(array, stream_key, smallest, largest):
    longest = array.shape.index(max(array.shape))
    spots = []
    for shift in (0, 1):
        where = [jax.random.randint(jax.random.fold_in(stream_key, axis), (), 0, length) for axis, length in enumerate(array.shape)]
        where[longest] = (where[longest] + shift) % array.shape[longest]
        spots.append(tuple(where))
    return array.at[spots[0]].set(smallest).at[spots[1]].set(largest)


def block_scale(key, extent, cuts, least, top_value):
    def one(dim, blocks):
        draws = jax.random.uniform(jax.random.fold_in(jax.random.fold_in(key, 6), dim), (blocks,), jnp.float32, least / len(cuts), top_value / len(cuts))
        return jnp.repeat(jnp.exp(draws), extent[dim] // blocks).reshape((-1,) + (1,) * (len(extent) - dim - 1))

    loudness = one(*cuts[0])
    for cut in cuts[1:]:
        loudness = loudness * one(*cut)
    return loudness


def centred(stream_key, extent, width, bound, cuts=(), kind=jnp.bfloat16):
    drawn = width * jax.random.normal(stream_key, extent, jnp.float32)
    if cuts:
        drawn = drawn * block_scale(stream_key, extent, cuts, -0.22, 0.18)
    return jnp.clip(drawn, -bound, bound).astype(kind)


def setup_inputs(seed: int = 0) -> dict:
    streams_of = jax.random.split(jax.random.key(seed), 9)
    return {
        "ensemble": centred(streams_of[0], (MEM, C, NLAT, NLON), 1.0, 6.0, ((0, 16), (2, 4), (3, 4))),
        "ancestry": draw_ancestry(jax.random.fold_in(streams_of[8], 71), 0),
        "obs_weights": jnp.clip(jnp.exp(math.log(10.0) - 4.6051702 * jax.random.uniform(streams_of[2], (MEM,), jnp.float32) ** block_scale(streams_of[2], (MEM,), ((0, 16),), -0.2, 0.2)), 0.1, 10.0),
        "kernel_index": with_ends(jax.random.randint(streams_of[3], (NLAT,), 0, KERN), jax.random.fold_in(streams_of[3], 1), 0, KERN - 1).astype(jnp.int32),
        "kernel_table": centred(streams_of[4], (KERN, 9, C), 0.5, 3.0, (), jnp.float32),
        "feature_scaling_factor": jnp.clip(1.0 + 0.18 * jax.random.normal(streams_of[5], (C,), jnp.float32), 0.1, 1.9),
        "entry_projection_matrix": centred(streams_of[6], (HID, C), C ** -0.5, 0.75),
        "exit_projection_matrix": centred(streams_of[7], (C, HID), HID ** -0.5, 0.15625),
    }


EPS = 1e-06

def finish(conv, field, feature_scaling_factor, entry_projection_matrix, exit_projection_matrix):
    mean_sq = lax.optimization_barrier(jnp.mean(conv * conv, axis=0))
    normed = (conv * lax.rsqrt(mean_sq + EPS) * feature_scaling_factor[:, None, None]).astype(jnp.bfloat16)
    flat = normed.reshape(normed.shape[0], -1)
    hidden = jax.nn.gelu(jnp.dot(entry_projection_matrix, flat, preferred_element_type=jnp.float32), approximate=True).astype(jnp.bfloat16)
    update = jnp.dot(exit_projection_matrix, hidden, preferred_element_type=jnp.float32) + field.reshape(field.shape[0], -1)
    return update.reshape(field.shape).astype(jnp.bfloat16)

def predict_once(particle_state, filter_coefficients, feature_scaling_factor, entry_projection_matrix, exit_projection_matrix):
    field = particle_state.astype(jnp.float32)
    row_count = field.shape[1]
    col_count = field.shape[2]
    padded = jnp.pad(field, ((0, 0), (1, 1), (0, 0)))
    padded = jnp.concatenate([padded[:, :, -1:], padded, padded[:, :, :1]], axis=2)
    conv = jnp.zeros_like(field)
    for tap_index in range(9):
        row_shift = tap_index // 3
        col_shift = tap_index % 3
        conv = conv + filter_coefficients[tap_index][:, :, None] * padded[:, row_shift:row_shift + row_count, col_shift:col_shift + col_count]
    return finish(conv, field, feature_scaling_factor, entry_projection_matrix, exit_projection_matrix)

def reference(ensemble, ancestry, obs_weights, kernel_index, kernel_table, feature_scaling_factor, entry_projection_matrix, exit_projection_matrix):
    filter_coefficients = jnp.transpose(jnp.take(kernel_table, kernel_index, axis=0), (1, 2, 0))
    redrawn_particles = jnp.take(ensemble, ancestry, axis=0)
    predicted_particles = lax.map(lambda particle_state: predict_once(particle_state, filter_coefficients, feature_scaling_factor, entry_projection_matrix, exit_projection_matrix), redrawn_particles)

    def accumulate(total, pair):
        weight, particle_state = pair
        return (total + weight * particle_state.astype(jnp.float32), None)
    start_total = jnp.zeros(ensemble.shape[1:], jnp.float32)
    weighted, _ = lax.scan(accumulate, start_total, (obs_weights, ensemble))
    importance_average_state = weighted / jnp.sum(obs_weights)
    return (predicted_particles, importance_average_state)
```

```python
import functools
import jax
import jax.numpy as jnp
from jax import lax
from jax.experimental import pallas as pl
from jax.experimental.pallas import tpu as pltpu
from jax.sharding import PartitionSpec as P

EPS = 1e-06
LANES = 128
CP = 80
GA = 0.7978845608028654
GB = GA * 0.044715
VM = pltpu.VMEM
SM = pltpu.SMEM
vspec = pl.BlockSpec(memory_space=VM)
sspec = pl.BlockSpec(memory_space=SM)


def cost(flops, nbytes):
    return pl.CostEstimate(flops=int(flops), bytes_accessed=int(nbytes), transcendentals=0)


def lanes_of(shape):
    return lax.broadcasted_iota(jnp.int32, shape, 1)


def prep_kernel(base, anc, ens, xt, top, bot, colw, cole, tab, flat, accw, acce, owner):
    mems, chans, rows, _ = ens.shape
    dests = mems

    def clear(k, carry):
        tab[k] = -1
        tab[mems + k] = -1
        owner[k] = -1
        return carry

    lax.fori_loop(0, mems, clear, 0, unroll=True)

    def find(q, carry):
        loc = anc[q] - base[0]

        @pl.when((loc >= 0) & (loc < mems))
        def _():
            tab[q // mems] = loc

        return carry

    lax.fori_loop(0, dests * mems, find, 0, unroll=8)

    def own(d, carry):
        m = tab[d]

        @pl.when(m >= 0)
        def _():
            @pl.when(owner[m] < 0)
            def _():
                owner[m] = d

            tab[mems + d] = owner[m]

        return carry

    lax.fori_loop(0, dests, own, 0)

    flat[pl.ds(chans * rows, (CP - chans) * rows), :] = jnp.zeros(
        ((CP - chans) * rows, LANES), jnp.float32
    )
    accw[...] = jnp.zeros_like(accw)
    acce[...] = jnp.zeros_like(acce)
    lane = lanes_of((CP, LANES))

    def member(d, carry):
        m = tab[d]

        @pl.when((m >= 0) & (tab[mems + d] == d))
        def _():
            flat[pl.ds(0, chans * rows), :] = (
                ens[m].astype(jnp.float32).reshape(chans * rows, LANES)
            )
            west = jnp.zeros((CP, LANES), jnp.float32)
            east = west
            for i in range(rows):
                row = flat[pl.ds(i, CP, stride=rows), :]
                low = row.astype(jnp.bfloat16)
                xt[m, i] = low
                if i == 0:
                    top[m] = low
                if i == rows - 1:
                    bot[m] = low
                west = jnp.where(lane == i, pltpu.roll(row, i, 1) if i else row, west)
                east = jnp.where(lane == i, pltpu.roll(row, i + 1, 1), east)
            mine = (lane // rows) == m
            accw[...] = jnp.where(mine, pltpu.roll(west, m * rows, 1), accw[...])
            acce[...] = jnp.where(mine, pltpu.roll(east, m * rows, 1), acce[...])

        return carry

    lax.fori_loop(0, dests, member, 0)
    colw[...] = accw[...].astype(jnp.bfloat16)
    cole[...] = acce[...].astype(jnp.bfloat16)


def prepare(base, ancestry, ensemble):
    mems, chans, rows, lanes = ensemble.shape
    sd = jax.ShapeDtypeStruct
    b = jnp.bfloat16
    return pl.pallas_call(
        prep_kernel,
        name="prep",
        in_specs=[sspec, sspec, vspec],
        out_specs=[vspec] * 5 + [sspec],
        out_shape=[
            sd((mems, rows, CP, lanes), b),
            sd((mems, CP, lanes), b),
            sd((mems, CP, lanes), b),
            sd((CP, lanes), b),
            sd((CP, lanes), b),
            sd((2 * mems,), jnp.int32),
        ],
        scratch_shapes=[
            VM((CP * rows, lanes), jnp.float32),
            VM((CP, lanes), jnp.float32),
            VM((CP, lanes), jnp.float32),
            SM((mems,), jnp.int32),
        ],
        cost_estimate=cost(4e6, 6e6),
    )(base, ancestry, ensemble)


def side_kernel(weights, kidx, ens, table, scale, sums, coef, mat):
    mems, chans, rows, _ = ens.shape
    pieces, depth, _ = sums.shape
    per = depth // rows - 1
    total = weights[0]
    for m in range(1, mems):
        total = total + weights[m]
    for piece in range(pieces):
        for k in range(per):
            c = piece * per + k
            if c < chans:
                acc = weights[0] * ens[0, c].astype(jnp.float32)
                for m in range(1, mems):
                    acc = acc + weights[m] * ens[m, c].astype(jnp.float32)
            else:
                acc = jnp.zeros((rows, LANES), jnp.float32)
            sums[piece, pl.ds(k * rows, rows), :] = acc
        sums[piece, pl.ds(per * rows, rows), :] = jnp.full((rows, LANES), total, jnp.float32)
    mat[...] = jnp.zeros_like(mat)
    taps = table.shape[1]
    for i in range(rows):
        for t in range(taps):
            mat[pl.ds(t * rows + i, 1), pl.ds(0, chans)] = table[kidx[i], pl.ds(t, 1), :]
    mat[pl.ds(taps * rows, 1), pl.ds(0, chans)] = scale[...]
    coef[...] = mat[...].T


def side(weights, kernel_index, ensemble, table, scale, pieces):
    mems, chans, rows, lanes = ensemble.shape
    per = -(-chans // pieces)
    return pl.pallas_call(
        side_kernel,
        name="side",
        in_specs=[sspec, sspec, vspec, vspec, vspec],
        out_specs=[vspec, vspec],
        out_shape=[
            jax.ShapeDtypeStruct((pieces, (per + 1) * rows, lanes), jnp.float32),
            jax.ShapeDtypeStruct((LANES, lanes), jnp.float32),
        ],
        scratch_shapes=[VM((LANES, lanes), jnp.float32)],
        cost_estimate=cost(4e6, 3e6),
    )(weights, kernel_index, ensemble, table, scale[None, :])


def mean_kernel(parts, out):
    pieces, depth, lanes = parts.shape
    rows = 8
    acc = parts[0]
    for k in range(1, pieces):
        acc = acc + parts[k]
    mean = acc[: depth - rows] / acc[depth - rows : depth - rows + 1]
    for k in range(pieces):
        out[k] = mean


def mean_piece(parts):
    pieces, depth, lanes = parts.shape
    return pl.pallas_call(
        mean_kernel,
        name="mean",
        in_specs=[vspec],
        out_specs=vspec,
        out_shape=jax.ShapeDtypeStruct((pieces, depth - 8, lanes), jnp.float32),
        cost_estimate=cost(1e5, 1e6),
    )(parts)


def forecast_kernel(chunk, chans, tab, xt, west, east, *rest):
    edges = len(rest) == 4 + 1 + 7
    if edges:
        north, south, cnorth, csouth = rest[:4]
        rest = rest[4:]
    coef, entry, exit_, send, taps, gain, conv, feed = rest
    mems, rows = xt.shape[:2]
    hid = entry.shape[0]
    body = chans - 1
    for k, i in enumerate(chunk):
        for t in range(9):
            lane = t * rows + i
            taps[k * 9 + t] = jnp.broadcast_to(coef[pl.ds(0, CP), lane : lane + 1], (CP, LANES))
    lane = 9 * rows
    gain[...] = jnp.broadcast_to(coef[pl.ds(0, CP), lane : lane + 1], (CP, LANES))
    step = 16
    lane = lanes_of((step, LANES))

    def source(m, a, s):
        at = pl.ds(s, step)
        if a < 0:
            x, w, e, spot = north[m, at], cnorth[0, at], cnorth[1, at], m * rows + rows - 1
        elif a >= rows:
            x, w, e, spot = south[m, at], csouth[0, at], csouth[1, at], m * rows
        else:
            x, w, e, spot = xt[m, a, at], west[at], east[at], m * rows + a
        x, w, e = (v.astype(jnp.float32) for v in (x, w, e))
        w = pltpu.roll(w, lax.rem(LANES - spot, LANES), 1)
        e = pltpu.roll(e, LANES - 1 - spot, 1)
        xw = jnp.where(lane == 0, w, pltpu.roll(x, 1, 1))
        xe = jnp.where(lane == LANES - 1, e, pltpu.roll(x, LANES - 1, 1))
        return xw, x, xe

    def one(d, carry):
        m = tab[d]
        owner = tab[mems + d]

        @pl.when((m >= 0) & (owner == d))
        def _():
            last = []
            for pair in range(0, len(chunk), 2):
                first = chunk[pair]
                ssq = [jnp.zeros((step, LANES), jnp.float32) for _ in range(2)]
                for s in range(0, CP, step):
                    got = {a: source(m, a, s) for a in range(first - 1, first + 3)}
                    for k in range(2):
                        acc = None
                        for t in range(9):
                            term = taps[(pair + k) * 9 + t, pl.ds(s, step)] * (
                                got[first + k + t // 3 - 1][t % 3]
                            )
                            acc = term if acc is None else acc + term
                        conv[k, pl.ds(s, step)] = acc
                        ssq[k] = ssq[k] + acc * acc
                for k in range(2):
                    mean = jnp.sum(ssq[k], axis=0, keepdims=True) * (1.0 / chans)
                    feed[:, pl.ds(k * LANES, LANES)] = (
                        conv[k] * lax.rsqrt(mean + EPS) * gain[...]
                    ).astype(jnp.bfloat16)
                x = feed[...]
                acc = None
                width = 256
                for h in range(0, hid, width):
                    v = jnp.dot(
                        entry[pl.ds(h, width), :], x, preferred_element_type=jnp.float32
                    )
                    g = v + v * jnp.tanh(v * (2 * GA + (8 * GB) * (v * v)))
                    part = jnp.dot(
                        exit_[:, pl.ds(h, width)],
                        g.astype(jnp.bfloat16),
                        preferred_element_type=jnp.float32,
                    )
                    acc = part if acc is None else acc + part
                for k in range(2):
                    new = acc[:, k * LANES : (k + 1) * LANES] + xt[m, first + k].astype(
                        jnp.float32
                    )
                    send[d, pl.ds((pair + k) * body, body), :] = new[:body].astype(jnp.bfloat16)
                    last.append(new[body : body + 1])
            pad = send.shape[1] - body * len(chunk) - len(chunk)
            last.append(jnp.zeros((pad, LANES), jnp.float32))
            send[d, pl.ds(body * len(chunk), len(chunk) + pad), :] = jnp.concatenate(
                last, axis=0
            ).astype(jnp.bfloat16)

        @pl.when((m >= 0) & (owner != d))
        def _():
            send[d] = send[owner]

        return carry

    lax.fori_loop(0, mems, one, 0)


def depth_of(chunk, chans):
    return -(-(chans * len(chunk)) // 8) * 8


def forecast(chunk, chans, tab, xt, west, east, edge, coef, entry, exit_):
    mems, rows, _, lanes = xt.shape
    hid = entry.shape[0]
    n = len(chunk)
    depth = depth_of(chunk, chans)
    args = (tab, xt, west, east, *edge, coef, entry, exit_)
    return pl.pallas_call(
        functools.partial(forecast_kernel, chunk, chans),
        name="forecast",
        in_specs=[sspec] + [vspec] * (len(args) - 1),
        out_specs=vspec,
        out_shape=jax.ShapeDtypeStruct((mems, depth, lanes), jnp.bfloat16),
        scratch_shapes=[
            VM((9 * n, CP, lanes), jnp.float32),
            VM((CP, lanes), jnp.float32),
            VM((2, CP, lanes), jnp.float32),
            VM((CP, 2 * lanes), jnp.bfloat16),
        ],
        cost_estimate=cost(2 * 2 * mems * hid * 256 * n * lanes, 8e6),
        compiler_params=pltpu.CompilerParams(vmem_limit_bytes=48 * 2**20),
    )(*args)


def gather_kernel(chunks, chans, base, anc, *refs):
    n = len(chunks)
    parts, out, flat = refs[:n], refs[n], refs[n + 1]
    rows = out.shape[2]
    body = chans - 1
    j = pl.program_id(0)
    src = anc[base[0] + j] // out.shape[0] if False else anc[base[0] + j] // pl.num_programs(0)
    for part, chunk in zip(parts, chunks):
        tail = part[src, pl.ds(body * len(chunk), part.shape[1] - body * len(chunk)), :].astype(
            jnp.float32
        )
        for k, i in enumerate(chunk):
            flat[pl.ds(i, body, stride=rows), :] = part[src, pl.ds(k * body, body), :].astype(
                jnp.float32
            )
            flat[pl.ds(body * rows + i, 1), :] = tail[k : k + 1]
    out[0] = flat[...].reshape(chans, rows, LANES).astype(jnp.bfloat16)


def gather(chunks, base, ancestry, parts, shape):
    mems, chans, rows, lanes = shape
    return pl.pallas_call(
        functools.partial(gather_kernel, chunks, chans),
        name="gather",
        grid=(mems,),
        in_specs=[sspec, sspec]
        + [pl.BlockSpec(p.shape, lambda j: (0, 0, 0), pipeline_mode=pl.Buffered(1)) for p in parts],
        out_specs=pl.BlockSpec((1, chans, rows, lanes), lambda j: (j, 0, 0, 0)),
        out_shape=jax.ShapeDtypeStruct(shape, jnp.bfloat16),
        scratch_shapes=[VM((chans * rows, lanes), jnp.float32)],
        cost_estimate=cost(4e6, 5e6),
    )(base, ancestry, *parts)


CHUNKS = ((2, 3), (4, 5, 0, 1, 6, 7))


def shards(
    ensemble,
    ancestry,
    obs_weights,
    kernel_index,
    kernel_table,
    feature_scaling_factor,
    entry_projection_matrix,
    exit_projection_matrix,
):
    mems, chans, rows, lanes = ensemble.shape
    count = lax.axis_size("mem")
    base = (lax.axis_index("mem") * mems).astype(jnp.int32).reshape(1)
    lat, lon = lax.axis_size("lat"), lax.axis_size("lon")
    up = [(i, i + 1) for i in range(lat - 1)]
    down = [(t, s) for s, t in up]
    right = [(i, (i + 1) % lon) for i in range(lon)]
    left = [(t, s) for s, t in right]

    xt, top, bot, colw, cole, tab = prepare(base, ancestry, ensemble)
    west = lax.ppermute(cole, "lon", right)
    east = lax.ppermute(colw, "lon", left)
    north = lax.ppermute(bot, "lat", up)
    south = lax.ppermute(top, "lat", down)
    both = jnp.stack([west, east])
    cnorth = lax.ppermute(both, "lat", up)
    csouth = lax.ppermute(both, "lat", down)

    sums, coef = side(
        obs_weights, kernel_index, ensemble, kernel_table, feature_scaling_factor, count
    )
    entry = jnp.pad(entry_projection_matrix, ((0, 0), (0, CP - chans))) * jnp.bfloat16(0.5)
    exit_ = jnp.pad(exit_projection_matrix, ((0, CP - chans), (0, 0)))

    swap = functools.partial(
        lax.all_to_all, axis_name="mem", split_axis=0, concat_axis=0, tiled=True
    )
    parts = swap(sums)
    got = []
    for chunk in CHUNKS:
        interior = all(0 < i < rows - 1 for i in chunk)
        edge = () if interior else (north, south, cnorth, csouth)
        sent = forecast(chunk, chans, tab, xt, west, east, edge, coef, entry, exit_)
        got.append(swap(sent))
    mean = swap(mean_piece(parts))
    importance = mean.reshape(-1, lanes)[: chans * rows].reshape(chans, rows, lanes)
    predicted = gather(CHUNKS, base, ancestry, got, ensemble.shape)
    return predicted, importance


def solution(mesh):
    return jax.shard_map(
        shards,
        mesh=mesh,
        in_specs=(P("mem", None, "lat", "lon"), P(), P("mem"), P("lat"), P(), P(), P(), P()),
        out_specs=(P("mem", None, "lat", "lon"), P(None, "lat", "lon")),
        check_vma=False,
    )
```

```python
import functools
import jax
import jax.numpy as jnp
from jax import lax
from jax.experimental import pallas as pl
from jax.experimental.pallas import tpu as pltpu
from jax.sharding import PartitionSpec as P

EPS = 1e-06
LANES = 128
BODY = 64
CP = 80
GA = 0.7978845608028654
GB = GA * 0.044715
VM = pltpu.VMEM
SM = pltpu.SMEM
vspec = pl.BlockSpec(memory_space=VM)
sspec = pl.BlockSpec(memory_space=SM)


def cost(flops, nbytes):
    return pl.CostEstimate(flops=int(flops), bytes_accessed=int(nbytes), transcendentals=0)


def lanes_of(shape):
    return lax.broadcasted_iota(jnp.int32, shape, 1)


def prep_kernel(base, anc, ens, xt, colw, cole, tab, flat, accw, acce, owner):
    mems, area, _ = ens.shape
    rows = xt.shape[1]
    chans = area // rows
    start = base[0]
    for m in range(mems):
        owner[m] = -1

    def find(d, carry):
        pick = jnp.int32(-1)
        for j in range(mems):
            loc = anc[d * mems + j] - start
            pick = jnp.where((loc >= 0) & (loc < mems), loc, pick)
        tab[d] = pick
        spot = jnp.maximum(pick, 0)
        had = owner[spot]
        mine = jnp.where(had < 0, d, had)
        tab[mems + d] = jnp.where(pick >= 0, mine, -1)
        owner[spot] = jnp.where(pick >= 0, mine, had)
        return carry

    lax.fori_loop(0, mems, find, 0)

    flat[pl.ds(chans * rows, (CP - chans) * rows), :] = jnp.zeros(
        ((CP - chans) * rows, LANES), jnp.float32
    )
    accw[...] = jnp.zeros_like(accw)
    acce[...] = jnp.zeros_like(acce)
    lane = lanes_of((CP, LANES))

    def member(d, carry):
        m = tab[d]

        @pl.when((m >= 0) & (tab[mems + d] == d))
        def _():
            flat[pl.ds(0, chans * rows), :] = ens[m].astype(jnp.float32)
            west = jnp.zeros((CP, LANES), jnp.float32)
            east = west
            for i in range(rows):
                row = flat[pl.ds(i, CP, stride=rows), :]
                xt[m, i] = row.astype(jnp.bfloat16)
                west = jnp.where(lane == i, pltpu.roll(row, i, 1) if i else row, west)
                east = jnp.where(lane == i, pltpu.roll(row, i + 1, 1), east)
            mine = (lane // rows) == m
            accw[...] = jnp.where(mine, pltpu.roll(west, m * rows, 1), accw[...])
            acce[...] = jnp.where(mine, pltpu.roll(east, m * rows, 1), acce[...])

        return carry

    lax.fori_loop(0, mems, member, 0)
    colw[...] = accw[...].astype(jnp.bfloat16)
    cole[...] = acce[...].astype(jnp.bfloat16)


def prepare(base, ancestry, ensemble, rows):
    mems, _, lanes = ensemble.shape
    sd = jax.ShapeDtypeStruct
    b = jnp.bfloat16
    return pl.pallas_call(
        prep_kernel,
        name="prep",
        in_specs=[sspec, sspec, vspec],
        out_specs=[vspec] * 3 + [sspec],
        out_shape=[
            sd((mems, rows, CP, lanes), b),
            sd((CP, lanes), b),
            sd((CP, lanes), b),
            sd((2 * mems,), jnp.int32),
        ],
        scratch_shapes=[
            VM((CP * rows, lanes), jnp.float32),
            VM((CP, lanes), jnp.float32),
            VM((CP, lanes), jnp.float32),
            SM((mems,), jnp.int32),
        ],
        cost_estimate=cost(4e6, 6e6),
    )(base, ancestry, ensemble)


def split(x):
    high = x.astype(jnp.bfloat16)
    return high, (x - high.astype(jnp.float32)).astype(jnp.bfloat16)


def side_kernel(weights, after, ens, sums):
    mems, area, _ = ens.shape
    pieces, depth, _ = sums.shape
    depth = depth // 2
    step = 16
    total = weights[0]
    for m in range(1, mems):
        total = total + weights[m]
    for piece in range(pieces):
        for k in range(0, depth, step):
            size = min(step, depth - k)
            at = piece * depth + k
            have = max(0, min(size, area - at))
            parts = []
            if have:
                acc = weights[0] * ens[0, pl.ds(at, have), :].astype(jnp.float32)
                for m in range(1, mems):
                    acc = acc + weights[m] * ens[m, pl.ds(at, have), :].astype(jnp.float32)
                parts.append(acc)
            if size - have:
                parts.append(jnp.zeros((size - have, LANES), jnp.float32))
            acc = jnp.concatenate(parts, axis=0) if len(parts) > 1 else parts[0]
            high, low = split(acc)
            sums[piece, pl.ds(k, size), :] = high
            sums[piece, pl.ds(depth + k, size), :] = low


def side(weights, after, ensemble, pieces):
    mems, area, lanes = ensemble.shape
    depth = -(-area // (8 * pieces)) * 8
    return pl.pallas_call(
        side_kernel,
        name="side",
        in_specs=[sspec, sspec, vspec],
        out_specs=vspec,
        out_shape=jax.ShapeDtypeStruct((pieces, 2 * depth, lanes), jnp.bfloat16),
        cost_estimate=cost(4e6, 3e6),
    )(weights, after, ensemble)


def attach_kernel(skip, base, parts, _, send, got, mean, sems):
    pieces, depth = parts.shape[0], got.shape[1] // 2 - 4
    load = pltpu.make_async_copy(parts.at[:, pl.ds(skip - 8, 2 * depth + 8)], got, sems.at[0])
    load.start()
    load.wait()
    acc = jnp.zeros((depth, LANES), jnp.float32)
    total = jnp.zeros((8, LANES), jnp.float32)
    for k in range(pieces):
        acc = acc + (
            got[k, pl.ds(8, depth), :].astype(jnp.float32)
            + got[k, pl.ds(8 + depth, depth), :].astype(jnp.float32)
        )
        total = total + got[k, pl.ds(0, 8), :].astype(jnp.float32)
    body = depth
    out = (acc / (total[4:5] + total[5:6])).astype(jnp.bfloat16)
    for k in range(pieces):
        mean[k] = out
    store = pltpu.make_async_copy(mean, send.at[:, pl.ds(base, body)], sems.at[1])
    store.start()
    store.wait()


def attach(skip, base, parts, send):
    pieces, depth, lanes = parts.shape
    anyspec = pl.BlockSpec(memory_space=pl.ANY)
    return pl.pallas_call(
        functools.partial(attach_kernel, skip, base),
        name="attach",
        in_specs=[anyspec, anyspec],
        out_specs=anyspec,
        out_shape=jax.ShapeDtypeStruct(send.shape, send.dtype),
        scratch_shapes=[
            VM((pieces, depth - skip + 8, lanes), jnp.bfloat16),
            VM((pieces, send.shape[1] - base, lanes), jnp.bfloat16),
            pltpu.SemaphoreType.DMA((2,)),
        ],
        input_output_aliases={1: 0},
        cost_estimate=cost(1e5, 1e6),
    )(parts, send)


def forecast_kernel(chunk, chans, first_chunk, tab, kidx, weights, xt, west, east, *rest):
    mems, rows = xt.shape[:2]
    send, upward, downward, copied = None, None, None, None
    if first_chunk:
        extra, table, scale, entry, exit_, send, upward, downward = rest[:8]
        sem = rest[8]
        rest = rest[9:]
    else:
        north, south, table, scale, entry, exit_, send = rest[:7]
        rest = rest[7:]
    mat, coef, taps, gain, conv, feed = rest
    hid = entry.shape[0]
    body = BODY
    base = depth_of(chunk, chans)
    total = jnp.float32(0)
    if first_chunk:
        copied = pltpu.make_async_copy(
            extra, send.at[:, pl.ds(base, send.shape[1] - base)], sem.at[0]
        )
        copied.start()
        for out, i in ((upward, rows - 1), (downward, 0)):
            for m in range(mems):
                out[m] = xt[m, i]
            out[mems] = west[...]
            out[mems + 1] = east[...]
        for m in range(mems):
            total = total + weights[m]
    high, low = split(jnp.full((1, LANES), total, jnp.float32))
    ends = jnp.concatenate(
        [high.astype(jnp.float32), low.astype(jnp.float32), jnp.zeros((2, LANES), jnp.float32)],
        axis=0,
    )
    mat[...] = jnp.zeros_like(mat)
    for k, i in enumerate(chunk):
        for t in range(9):
            mat[pl.ds(k * 9 + t, 1), pl.ds(0, chans)] = table[kidx[i], pl.ds(t, 1), :]
    spare = 9 * len(chunk)
    mat[pl.ds(spare, 1), pl.ds(0, chans)] = scale[...]
    coef[...] = mat[...].T
    for lane in range(spare):
        taps[lane] = jnp.broadcast_to(coef[pl.ds(0, CP), lane : lane + 1], (CP, LANES))
    gain[...] = jnp.broadcast_to(coef[pl.ds(0, CP), spare : spare + 1], (CP, LANES))
    step = 16
    lane = lanes_of((step, LANES))

    def source(m, a, s):
        at = pl.ds(s, step)
        if a < 0:
            x, w, e, spot = north[m, at], north[mems, at], north[mems + 1, at], m * rows + rows - 1
        elif a >= rows:
            x, w, e, spot = south[m, at], south[mems, at], south[mems + 1, at], m * rows
        else:
            x, w, e, spot = xt[m, a, at], west[at], east[at], m * rows + a
        x, w, e = (v.astype(jnp.float32) for v in (x, w, e))
        w = pltpu.roll(w, lax.rem(LANES - spot, LANES), 1)
        e = pltpu.roll(e, LANES - 1 - spot, 1)
        xw = jnp.where(lane == 0, w, pltpu.roll(x, 1, 1))
        xe = jnp.where(lane == LANES - 1, e, pltpu.roll(x, LANES - 1, 1))
        return xw, x, xe

    def one(d, carry):
        m = tab[d]
        owner = tab[mems + d]

        @pl.when((m >= 0) & (owner == d))
        def _():
            mid, last = [], []
            for pair in range(0, len(chunk), 2):
                first = chunk[pair]
                ssq = [jnp.zeros((step, LANES), jnp.float32) for _ in range(2)]
                for s in range(0, CP, step):
                    got = {a: source(m, a, s) for a in range(first - 1, first + 3)}
                    for k in range(2):
                        acc = None
                        for t in range(9):
                            term = taps[(pair + k) * 9 + t, pl.ds(s, step)] * (
                                got[first + k + t // 3 - 1][t % 3]
                            )
                            acc = term if acc is None else acc + term
                        conv[pair + k, pl.ds(s, step)] = acc
                        ssq[k] = ssq[k] + acc * acc
                for k in range(2):
                    mean = jnp.sum(ssq[k], axis=0, keepdims=True) * (1.0 / chans)
                    feed[pair // 2, :, pl.ds(k * LANES, LANES)] = (
                        conv[pair + k] * lax.rsqrt(mean + EPS) * gain[...]
                    ).astype(jnp.bfloat16)
            for pair in range(0, len(chunk), 2):
                first = chunk[pair]
                x = feed[pair // 2]
                acc = None
                width = 256
                for h in range(0, hid, width):
                    v = jnp.dot(
                        entry[pl.ds(h, width), :], x, preferred_element_type=jnp.float32
                    )
                    g = (v + v * jnp.tanh(v * (2 * GA + (8 * GB) * (v * v)))).astype(jnp.bfloat16)
                    part = jnp.dot(
                        exit_[:, pl.ds(h, width)], g, preferred_element_type=jnp.float32
                    )
                    acc = part if acc is None else acc + part
                for k in range(2):
                    new = acc[:, k * LANES : (k + 1) * LANES] + xt[m, first + k].astype(
                        jnp.float32
                    )
                    send[d, pl.ds((pair + k) * body, body), :] = new[:body].astype(jnp.bfloat16)
                    mid.append(new[body : chans - 1])
                    last.append(new[chans - 1 : chans])
            n = len(chunk)
            send[d, pl.ds(body * n, base - body * n), :] = jnp.concatenate(
                mid + last + [ends], axis=0
            ).astype(jnp.bfloat16)

        @pl.when((m >= 0) & (owner != d))
        def _():
            send[d, pl.ds(0, base), :] = send[owner, pl.ds(0, base), :]

        if first_chunk:

            @pl.when(m < 0)
            def _():
                send[d, pl.ds(base - 8, 8), :] = jnp.concatenate(
                    [jnp.zeros((4, LANES), jnp.float32), ends], axis=0
                ).astype(jnp.bfloat16)

        return carry

    lax.fori_loop(0, mems, one, 0)
    if first_chunk:
        copied.wait()


def depth_of(chunk, chans):
    return -(-(chans * len(chunk)) // 8) * 8


def forecast(chunk, chans, small, tab, xt, west, east, edge, extra):
    kidx, weights, table, scale, entry, exit_ = small
    mems, rows, _, lanes = xt.shape
    hid = entry.shape[0]
    n = len(chunk)
    first = not edge
    anyspec = pl.BlockSpec(memory_space=pl.ANY)
    if first:
        edge, more, specs = (extra,), extra.shape[1], [anyspec]
    else:
        more, specs = extra, [vspec] * 2
    depth = depth_of(chunk, chans) + more
    args = (tab, kidx, weights, xt, west, east, *edge, table, scale, entry, exit_)
    sd = jax.ShapeDtypeStruct
    outs = [sd((mems, depth, lanes), jnp.bfloat16)]
    if first:
        outs += [sd((mems + 2, CP, lanes), jnp.bfloat16)] * 2
    return pl.pallas_call(
        functools.partial(forecast_kernel, chunk, chans, first),
        name="forecast",
        in_specs=[sspec] * 3 + [vspec] * 3 + specs + [vspec] * 4,
        out_specs=[vspec] * len(outs),
        out_shape=outs,
        scratch_shapes=([pltpu.SemaphoreType.DMA((1,))] if first else [])
        + [
            VM((LANES, lanes), jnp.float32),
            VM((LANES, lanes), jnp.float32),
            VM((9 * n, CP, lanes), jnp.float32),
            VM((CP, lanes), jnp.float32),
            VM((n, CP, lanes), jnp.float32),
            VM((n // 2, CP, 2 * lanes), jnp.bfloat16),
        ],
        cost_estimate=cost(2 * 2 * mems * hid * 256 * n * lanes, 8e6),
        compiler_params=pltpu.CompilerParams(vmem_limit_bytes=48 * 2**20),
    )(*args)


def gather_kernel(chunks, chans, base, anc, *refs):
    n = len(chunks)
    parts, out, importance, flat = refs[:n], refs[n], refs[n + 1], refs[n + 2]
    rows = out.shape[1] // chans
    j = pl.program_id(0)
    src = anc[base[0] + j] // pl.num_programs(0)
    for part, chunk in zip(parts, chunks):
        depth, size = depth_of(chunk, chans), len(chunk)
        tail = part[src, pl.ds(BODY * size, depth - BODY * size), :].astype(jnp.float32)
        mid = chans - 1 - BODY
        for k, i in enumerate(chunk):
            flat[pl.ds(i, BODY, stride=rows), :] = part[src, pl.ds(k * BODY, BODY), :].astype(
                jnp.float32
            )
            flat[pl.ds(BODY * rows + i, mid, stride=rows), :] = tail[k * mid : (k + 1) * mid]
            flat[pl.ds((chans - 1) * rows + i, 1), :] = tail[mid * size + k : mid * size + k + 1]
    out[0] = flat[...].astype(jnp.bfloat16)

    @pl.when(j == 0)
    def _():
        last = parts[-1]
        skip = depth_of(chunks[-1], chans)
        per = last.shape[1] - skip
        area = chans * rows
        for p in range(last.shape[0]):
            size = min(per, area - p * per)
            if size > 0:
                importance[pl.ds(p * per, size), :] = last[p, pl.ds(skip, size), :].astype(
                    jnp.float32
                )


def gather(chunks, base, ancestry, parts, shape):
    mems, chans, rows, lanes = shape
    area = chans * rows
    predicted, importance = pl.pallas_call(
        functools.partial(gather_kernel, chunks, chans),
        name="gather",
        grid=(mems,),
        in_specs=[sspec, sspec]
        + [pl.BlockSpec(p.shape, lambda j: (0, 0, 0), pipeline_mode=pl.Buffered(1)) for p in parts],
        out_specs=[
            pl.BlockSpec((1, area, lanes), lambda j: (j, 0, 0)),
            pl.BlockSpec((area, lanes), lambda j: (0, 0)),
        ],
        out_shape=[
            jax.ShapeDtypeStruct((mems, area, lanes), jnp.bfloat16),
            jax.ShapeDtypeStruct((area, lanes), jnp.float32),
        ],
        scratch_shapes=[VM((area, lanes), jnp.float32)],
        cost_estimate=cost(4e6, 5e6),
    )(base, ancestry, *parts)
    return predicted.reshape(shape), importance.reshape(shape[1:])


CHUNKS = ((2, 3, 4, 5), (0, 1, 6, 7))


def shards(
    ensemble,
    ancestry,
    obs_weights,
    kernel_index,
    kernel_table,
    feature_scaling_factor,
    entry_projection_matrix,
    exit_projection_matrix,
):
    mems, chans, rows, lanes = ensemble.shape
    count = lax.axis_size("mem")
    base = (lax.axis_index("mem") * mems).astype(jnp.int32).reshape(1)
    lat, lon = lax.axis_size("lat"), lax.axis_size("lon")
    up = [(i, i + 1) for i in range(lat - 1)]
    down = [(t, s) for s, t in up]
    right = [(i, (i + 1) % lon) for i in range(lon)]
    left = [(t, s) for s, t in right]
    swap = functools.partial(
        lax.all_to_all, axis_name="mem", split_axis=0, concat_axis=0, tiled=True
    )

    flat = ensemble.reshape(mems, chans * rows, lanes)
    xt, colw, cole, tab = prepare(base, ancestry, flat, rows)
    west = lax.ppermute(cole, "lon", right)
    east = lax.ppermute(colw, "lon", left)
    sums = side(obs_weights, tab, flat, count)
    entry = jnp.pad(entry_projection_matrix, ((0, 0), (0, CP - chans))) * jnp.bfloat16(0.5)
    exit_ = jnp.pad(exit_projection_matrix, ((0, CP - chans), (0, 0)))
    small = (
        kernel_index,
        obs_weights,
        kernel_table,
        feature_scaling_factor[None, :],
        entry,
        exit_,
    )

    inner, outer = CHUNKS
    sent, upward, downward = forecast(inner, chans, small, tab, xt, west, east, (), sums)
    north = lax.ppermute(upward, "lat", up)
    south = lax.ppermute(downward, "lat", down)
    got_inner = swap(sent)
    (sent,) = forecast(
        outer, chans, small, tab, xt, west, east, (north, south), sums.shape[1] // 2
    )
    sent = attach(depth_of(inner, chans), depth_of(outer, chans), got_inner, sent)
    got_outer = swap(sent)
    return gather(CHUNKS, base, ancestry, (got_inner, got_outer), ensemble.shape)


def solution(mesh):
    return jax.shard_map(
        shards,
        mesh=mesh,
        in_specs=(P("mem", None, "lat", "lon"), P(), P("mem"), P("lat"), P(), P(), P(), P()),
        out_specs=(P("mem", None, "lat", "lon"), P(None, "lat", "lon")),
        check_vma=False,
    )
```
